32 devices in a mesh: expert: 16 (over z, x, core), tensor: 2 (over y).
Axes of the slice: x: 2, y: 2, z: 4, core: 2. Of those that a mesh axis runs over, the one named last changes fastest.
Arguments:
- query: bfloat16 [128, 8192], P(('expert', 'tensor')), may hold values from -6 to 6
- cache_keys: bfloat16 [128, 128, 4, 128], P(('expert', 'tensor')), may hold values from -6 to 6
- cache_values: bfloat16 [128, 128, 4, 128], P(('expert', 'tensor')), may hold values from -6 to 6
- lengths: int32 [128], P(('expert', 'tensor')), may hold values from 2 to 128, as said below
- residual: bfloat16 [128, 4096], P('tensor', 'expert'), may hold values from -12 to 12
- out_proj: bfloat16 [4096, 8192], P('expert', 'tensor'), may hold values from -0.0625 to 0.0625
- norm_gain: bfloat16 [4096], P('expert'), may hold values from 0.099609375 to 1.8984375
- expert_ids: int32 [128, 8], replicated, may hold values from 0 to 15, all different within a row; in each aligned block of 128 rows (0 to 127, 128 to 255, ...) at most 128 rows name the same one
- gate_scores: bfloat16 [128, 8], replicated, may hold values from 0.019897461 to 1
- w_gate: bfloat16 [16, 1536, 4096], P('expert', 'tensor'), may hold values from -0.09375 to 0.09375
- w_up: bfloat16 [16, 1536, 4096], P('expert', 'tensor'), may hold values from -0.09375 to 0.09375
- w_down: bfloat16 [16, 1536, 4096], P('expert', 'tensor'), may hold values from -0.15625 to 0.15625
Outputs:
- attn_residual: bfloat16 [128, 4096], P('tensor', 'expert')
- expert_mix: bfloat16 [128, 4096], P('tensor', 'expert')
The draws below stay inside these ranges and needn't reach their ends.
Inputs may be any that keep to these rules, and one draw needn't show every extreme that they name: `expert_ids`: each row names 8 different experts; no expert is named by more than 128 rows, and one by exactly 128. `lengths`: some row has exactly 128.
All inputs are finite; a program needn't handle non-finite values.
Results may differ from the reference program's by a relative error of at most 0.018.
Values may be sent and summed in bfloat16 or wider, within the bound.
A program may use at most 64 MiB of HBM per device.

```python
import math
import jax
import jax.numpy as jnp
import numpy as np
from jax import lax

D = 4096
HEADS = 64
KV_HEADS = 4
HEAD_DIM = 128
FF = 1536
TOPK = 8
CACHE = 128
ROWS = 128
EXPERTS = 16
CAP = 128


def draw_query(key, part):
    blended = jnp.clip(jax.random.normal(jax.random.fold_in(key, 11), (ROWS, HEADS, HEAD_DIM), jnp.float32), -6.0, 6.0)
    return blended.reshape(ROWS, HEADS * HEAD_DIM).astype(jnp.bfloat16)


def draw_cache_keys(key, part):
    key_shape = (ROWS, CACHE, KV_HEADS, HEAD_DIM)
    drawn_draw = jnp.clip(jax.random.normal(jax.random.fold_in(key, 12), key_shape, jnp.float32), -6.0, 6.0)
    return drawn_draw.astype(jnp.bfloat16)


def draw_lengths(key, part):
    drawn = jax.random.randint(jax.random.fold_in(key, 21), (ROWS,), 2, CACHE + 1, dtype=jnp.int32)
    marked = jax.random.randint(jax.random.fold_in(key, 22), (), 0, ROWS, dtype=jnp.int32)
    return jnp.where(jnp.arange(ROWS, dtype=jnp.int32) == marked, CACHE, drawn).astype(jnp.int32)


def draw_residual(key, part):
    rising = 3.0 ** (jnp.arange(D, dtype=jnp.float32) / D)
    column_scale = jnp.exp(jax.random.uniform(jax.random.fold_in(key, 31), (D,), jnp.float32, 0.0, math.log(3.0)))
    base_draw = jnp.clip(jax.random.normal(jax.random.fold_in(key, 32), (ROWS, D), jnp.float32), -5.0, 5.0)
    row_scale = jnp.exp(jax.random.uniform(jax.random.fold_in(key, 34), (ROWS, 1), jnp.float32, math.log(0.3), math.log(3.0)))
    drawn = base_draw * rising[None, :] * column_scale[None, :] * row_scale * 0.3
    return jnp.clip(drawn, -12.0, 12.0).astype(jnp.bfloat16)


def steps_of(key, extent, cuts, least, high):
    gain = 1.0
    for position, blocks in cuts:
        draws = jax.random.uniform(jax.random.fold_in(jax.random.fold_in(key, 6), position), (blocks,), jnp.float32, least / len(cuts), high / len(cuts))
        gain = gain * jnp.repeat(jnp.exp(draws), extent[position] // blocks).reshape((-1,) + (1,) * (len(extent) - 1 - position))
    return gain


def assign_block(stream_key, own, number, rows, amount, top, bound, skew):
    order = jax.random.permutation(stream_key, amount)
    heavy_load, usual = load_shares(amount, rows * top, bound, skew, True), load_shares(amount, rows * top, bound, skew, False)
    places = jnp.arange(amount)

    def named(sizes, rotation):
        used = int((sizes > 0).sum())
        fixed = max(1, used // 4)
        passed = fixed + (places - fixed + rotation * (used - fixed)) % max(1, amount - fixed)
        return jnp.zeros((amount,), jnp.int32).at[order[jnp.where(places < fixed, places, passed)]].set(jnp.asarray(sizes, jnp.int32))

    sizes = jnp.where(number % 4 == 0, named(heavy_load, number // 4), named(usual, number - number // 4 - 1))
    mixed = jax.random.permutation(jax.random.fold_in(own, 3), amount)
    giver, sink = mixed[0:amount // 2 * 2:2], mixed[1:amount // 2 * 2:2]
    margin = jnp.minimum(sizes[giver] - 1, bound - sizes[sink]) // 2
    margin = jnp.where((giver == order[0]) | (sink == order[0]) | (sizes[sink] == 0), 0, jnp.maximum(margin, 0))
    passed = jax.random.randint(jax.random.fold_in(own, 4), (amount // 2,), 0, 1 << 20) % (margin + 1)
    sizes = sizes.at[giver].add(-passed).at[sink].add(passed)
    members = jnp.searchsorted(jnp.cumsum(sizes), jnp.arange(rows * top), side="right").astype(jnp.int32)
    listing = members.reshape(top, rows).T
    listing = listing[jax.random.permutation(jax.random.fold_in(own, 1), rows)]
    rotation = jax.random.randint(jax.random.fold_in(own, 2), (rows, 1), 0, top)
    return jnp.take_along_axis(listing, (jnp.arange(top)[None, :] + rotation) % top, axis=1)


def load_shares(number_of, total, reach, slope, full):
    loads = [(1 << 20) // math.isqrt(standing ** slope) + 1 for standing in range(1, number_of + 1)]
    largest = reach if full else min(reach, max(-(-total // number_of), total * loads[0] // sum(loads)))
    least = 1 if total - largest >= number_of - 1 else 0
    counts, rest = [largest] + [least] * (number_of - 1), total - largest - least * (number_of - 1)
    while rest > 0:
        free = [i for i in range(1, number_of) if counts[i] < largest] or [i for i in range(1, number_of) if counts[i] < reach]
        pool, remaining = sum([loads[i] for i in free]), rest
        for i in free:
            extra = min(reach - counts[i], max(1, remaining * loads[i] // pool), rest)
            counts[i] = counts[i] + extra
            rest = rest - extra
    return np.array(counts)


def scatter_about(key, dims, deviation, most, shards=(), kind=jnp.bfloat16):
    values = jax.random.normal(key, dims, jnp.float32) * deviation
    if len(shards) > 0:
        values = steps_of(key, dims, shards, -0.22, 0.18) * values
    return jnp.clip(values, min=-most, max=most).astype(kind)


def setup_inputs(seed: int = 0) -> dict:
    arg_keys = jax.random.split(jax.random.key(seed), 13)
    query = draw_query(jax.random.fold_in(arg_keys[12], 71), 0)
    cache_keys = draw_cache_keys(jax.random.fold_in(arg_keys[12], 71), 0)
    cache_values = scatter_about(arg_keys[2], (ROWS, CACHE, KV_HEADS, HEAD_DIM), 1.0, 6.0, ((0, 32),))
    lengths = draw_lengths(jax.random.fold_in(arg_keys[12], 71), 0)
    residual = draw_residual(jax.random.fold_in(arg_keys[12], 71), 0)
    out_proj = scatter_about(arg_keys[5], (D, HEADS * HEAD_DIM), (HEADS * HEAD_DIM) ** -0.5, 0.0625, ((0, 16), (1, 2)))
    norm_gain = jnp.clip(1.0 + 0.18 * jax.random.normal(arg_keys[6], (D,), jnp.float32), 0.099609375, 1.8984375).astype(jnp.bfloat16)
    expert_ids_keys = jax.random.split(jax.random.fold_in(arg_keys[7], 1), ROWS // ROWS)
    expert_ids_turns = jax.random.permutation(jax.random.fold_in(arg_keys[7], 3), ROWS // ROWS)
    expert_ids = jax.vmap(lambda own, number: assign_block(jax.random.fold_in(arg_keys[7], 2), own, number, ROWS, EXPERTS, TOPK, CAP, 2))(expert_ids_keys, expert_ids_turns).reshape((ROWS, TOPK))
    gate_scores = jnp.clip(jnp.exp(jax.random.uniform(arg_keys[8], (ROWS, TOPK), jnp.float32, math.log(0.019897461), math.log(1.0))), 0.019897461, 1.0).astype(jnp.bfloat16)
    w_gate = scatter_about(arg_keys[9], (EXPERTS, FF, D), D ** -0.5, 0.09375, ((0, 16), (1, 2)))
    w_up = scatter_about(arg_keys[10], (EXPERTS, FF, D), D ** -0.5, 0.09375, ((0, 16), (1, 2)))
    w_down = scatter_about(arg_keys[11], (EXPERTS, FF, D), FF ** -0.5, 0.15625, ((0, 16), (1, 2)))
    return dict(query=query, cache_keys=cache_keys, cache_values=cache_values, lengths=lengths, residual=residual, out_proj=out_proj, norm_gain=norm_gain, expert_ids=expert_ids, gate_scores=gate_scores, w_gate=w_gate, w_up=w_up, w_down=w_down)


def reference(query, cache_keys, cache_values, lengths, residual, out_proj, norm_gain, expert_ids, gate_scores, w_gate, w_up, w_down):
    group_size = HEADS // KV_HEADS
    grouped = query.astype(jnp.float32).reshape(ROWS, KV_HEADS, group_size, HEAD_DIM)
    scores = jnp.einsum('rkgd,rpkd->rkgp', grouped, cache_keys.astype(jnp.float32)) * HEAD_DIM ** (-0.5)
    usable = jnp.arange(CACHE, dtype=jnp.int32)[None, :] < lengths[:, None]
    usable_mask = usable[:, None, None, :]
    peak = lax.optimization_barrier(jnp.max(jnp.where(usable_mask, scores, -jnp.inf), axis=-1, keepdims=True))
    raw_weights = jnp.where(usable_mask, jnp.exp(scores - peak), 0.0)
    attn_weights = raw_weights / lax.optimization_barrier(jnp.sum(raw_weights, axis=-1, keepdims=True))
    context = jnp.einsum('rkgp,rpkd->rkgd', attn_weights, cache_values.astype(jnp.float32))
    context = context.reshape(ROWS, HEADS * HEAD_DIM).astype(jnp.bfloat16)
    attn_out = jnp.dot(context, out_proj.T, preferred_element_type=jnp.float32)
    hidden_state = residual.astype(jnp.float32) + attn_out
    mean_square = lax.optimization_barrier(jnp.mean(hidden_state * hidden_state, axis=1, keepdims=True))
    normed = (hidden_state * lax.rsqrt(mean_square + 1e-06) * norm_gain.astype(jnp.float32)[None, :]).astype(jnp.bfloat16)
    gate_weight = gate_scores.astype(jnp.float32)
    gate_weight = gate_weight / lax.optimization_barrier(jnp.sum(gate_weight, axis=1, keepdims=True))
    flat_ids = expert_ids.reshape(-1).astype(jnp.int32)
    onehot = (flat_ids[:, None] == jnp.arange(EXPERTS, dtype=jnp.int32)[None, :]).astype(jnp.int32)
    slot_index = lax.optimization_barrier(jnp.sum((jnp.cumsum(onehot, axis=0) - onehot) * onehot, axis=1)).astype(jnp.int32)
    destination = (flat_ids * CAP + slot_index).astype(jnp.int32)
    source = (jnp.arange(ROWS * TOPK, dtype=jnp.int32) // TOPK).astype(jnp.int32)
    slot_owner = jnp.full((EXPERTS * CAP,), -1, jnp.int32).at[destination].set(source).reshape(EXPERTS, CAP)

    def expert_block(pieces):
        owners, gate_mat, up_mat, down_mat = pieces
        rows_in = jnp.where((owners >= 0)[:, None], normed[jnp.maximum(owners, 0)], jnp.zeros((), jnp.bfloat16))
        gate_proj = jnp.dot(rows_in, gate_mat.T, preferred_element_type=jnp.float32)
        up_proj = jnp.dot(rows_in, up_mat.T, preferred_element_type=jnp.float32)
        activation = (jax.nn.silu(gate_proj) * up_proj).astype(jnp.bfloat16)
        return jnp.dot(activation, down_mat, preferred_element_type=jnp.float32)
    expert_result = lax.map(expert_block, (slot_owner, w_gate, w_up, w_down))
    picked = expert_result.reshape(EXPERTS * CAP, D)[destination].reshape(ROWS, TOPK, D)
    expert_mix = lax.optimization_barrier(jnp.sum(picked * gate_weight[:, :, None], axis=1)).astype(jnp.bfloat16)
    return (hidden_state.astype(jnp.bfloat16), expert_mix)
```

```python
import jax
import jax.numpy as jnp
from jax import lax
from jax.sharding import PartitionSpec as P

floor_value = -1e30
epsilon = 1e-06


def softmax_parts(queries, key_block, value_block, usable, score_scale):
    scores = (
        jnp.einsum("rkgd,rpkd->rkgp", queries, key_block, preferred_element_type=jnp.float32)
        * score_scale
    )
    usable_mask = usable[:, None, None, :]
    peak = jnp.max(jnp.where(usable_mask, scores, floor_value), axis=-1)
    raw_weights = jnp.where(usable_mask, jnp.exp(scores - peak[..., None]), 0.0)
    weight_sum = jnp.sum(raw_weights, axis=-1)
    weighted = jnp.einsum("rkgp,rpkd->rkgd", raw_weights, value_block.astype(jnp.float32))
    return (weight_sum, weighted)


def body(
    query,
    cache_keys,
    cache_values,
    lengths,
    residual,
    out_proj,
    norm_gain,
    expert_ids,
    gate_scores,
    w_gate,
    w_up,
    w_down,
):
    row_count, full_heads_width = query.shape
    cache_len = cache_keys.shape[1]
    kv_count = cache_keys.shape[2]
    head_size = cache_keys.shape[3]
    head_count = full_heads_width // head_size
    group_size = head_count // kv_count
    score_scale = head_size ** (-0.5)
    usable = jnp.arange(cache_len, dtype=jnp.int32)[None, :] < lengths[:, None]
    grouped = query.reshape(row_count, kv_count, group_size, head_size)
    weight_sum, weighted = softmax_parts(grouped, cache_keys, cache_values, usable, score_scale)
    context_rows_own = (
        (weighted / weight_sum[..., None]).astype(jnp.bfloat16).reshape(row_count, full_heads_width)
    )
    context = lax.all_to_all(context_rows_own, "tensor", split_axis=1, concat_axis=0, tiled=True)
    attn_part = jnp.dot(
        lax.all_gather(context, "expert", axis=0, tiled=True),
        out_proj.T,
        preferred_element_type=jnp.float32,
    )
    attn_share = lax.psum_scatter(attn_part, "tensor", scatter_dimension=0, tiled=True)
    hidden_state = residual.astype(jnp.float32) + attn_share
    squares = lax.psum(jnp.sum(hidden_state * hidden_state, axis=1), "expert")
    full_width = hidden_state.shape[1] * lax.axis_size("expert")
    scaled_share = (hidden_state * norm_gain.astype(jnp.float32)[None, :]).astype(jnp.bfloat16)
    scaled = lax.all_gather(
        lax.all_gather(scaled_share, "tensor", axis=0, tiled=True), "expert", axis=1, tiled=True
    )
    mean_all = lax.all_gather(squares / full_width, "tensor", axis=0, tiled=True)
    row_scale = lax.rsqrt(mean_all + epsilon)[:, None]
    experts_local = w_gate.shape[0]
    gate_weight = gate_scores.astype(jnp.float32)
    gate_weight = gate_weight / jnp.sum(gate_weight, axis=1, keepdims=True)
    mixed = None
    for local in range(experts_local):
        expert = lax.axis_index("expert") * experts_local + local
        weight = jnp.sum(jnp.where(expert_ids == expert, gate_weight, 0.0), axis=1, keepdims=True)
        gate_proj = row_scale * lax.dot_general(
            scaled, w_gate[local], (((1,), (1,)), ((), ())), preferred_element_type=jnp.float32
        )
        up_proj = row_scale * lax.dot_general(
            scaled, w_up[local], (((1,), (1,)), ((), ())), preferred_element_type=jnp.float32
        )
        activation = (jax.nn.silu(gate_proj) * up_proj).astype(jnp.bfloat16)
        part = weight * jnp.dot(activation, w_down[local], preferred_element_type=jnp.float32)
        mixed = part if mixed is None else mixed + part
    mixed = lax.psum_scatter(
        mixed.astype(jnp.bfloat16), "tensor", scatter_dimension=0, tiled=True
    )
    mixed_share = lax.psum_scatter(mixed, "expert", scatter_dimension=1, tiled=True)
    return (hidden_state.astype(jnp.bfloat16), mixed_share)


def solution(mesh):
    in_specs = (
        P(("expert", "tensor"), None),
        P(("expert", "tensor"), None, None, None),
        P(("expert", "tensor"), None, None, None),
        P(("expert", "tensor")),
        P("tensor", "expert"),
        P("expert", "tensor"),
        P("expert"),
        P(),
        P(),
        P("expert", "tensor", None),
        P("expert", "tensor", None),
        P("expert", "tensor", None),
    )
    out_specs = (P("tensor", "expert"), P("tensor", "expert"))
    return jax.shard_map(body, mesh=mesh, in_specs=in_specs, out_specs=out_specs, check_vma=False)
```

```python
import jax
import jax.numpy as jnp
from jax import lax
from jax.experimental import pallas as pl
from jax.experimental.pallas import tpu as pltpu
from jax.sharding import PartitionSpec as P

floor_value = -1e30
epsilon = 1e-06


def softmax_parts(queries, key_block, value_block, usable, score_scale):
    scores = (
        jnp.einsum("rkgd,rpkd->rkgp", queries, key_block, preferred_element_type=jnp.float32)
        * score_scale
    )
    usable_mask = usable[:, None, None, :]
    peak = jnp.max(jnp.where(usable_mask, scores, floor_value), axis=-1)
    raw_weights = jnp.where(usable_mask, jnp.exp(scores - peak[..., None]), 0.0)
    weight_sum = jnp.sum(raw_weights, axis=-1)
    weighted = jnp.einsum("rkgp,rpkd->rkgd", raw_weights, value_block.astype(jnp.float32))
    return (weight_sum, weighted)


def body(
    query,
    cache_keys,
    cache_values,
    lengths,
    residual,
    out_proj,
    norm_gain,
    expert_ids,
    gate_scores,
    w_gate,
    w_up,
    w_down,
):
    row_count, full_heads_width = query.shape
    cache_len = cache_keys.shape[1]
    kv_count = cache_keys.shape[2]
    head_size = cache_keys.shape[3]
    head_count = full_heads_width // head_size
    group_size = head_count // kv_count
    score_scale = head_size ** (-0.5)
    usable = jnp.arange(cache_len, dtype=jnp.int32)[None, :] < lengths[:, None]
    grouped = query.reshape(row_count, kv_count, group_size, head_size)
    weight_sum, weighted = softmax_parts(grouped, cache_keys, cache_values, usable, score_scale)
    context_rows_own = (
        (weighted / weight_sum[..., None]).astype(jnp.bfloat16).reshape(row_count, full_heads_width)
    )
    context = lax.all_to_all(context_rows_own, "tensor", split_axis=1, concat_axis=0, tiled=True)
    attn_part = jnp.dot(
        lax.all_gather(context, "expert", axis=0, tiled=True),
        out_proj.T,
        preferred_element_type=jnp.float32,
    )
    attn_share = lax.psum_scatter(attn_part, "tensor", scatter_dimension=0, tiled=True)
    hidden_state = residual.astype(jnp.float32) + attn_share
    squares = lax.psum(jnp.sum(hidden_state * hidden_state, axis=1), "expert")
    full_width = hidden_state.shape[1] * lax.axis_size("expert")
    scaled_share = (hidden_state * norm_gain.astype(jnp.float32)[None, :]).astype(jnp.bfloat16)
    scaled = lax.all_gather(
        lax.all_gather(scaled_share, "tensor", axis=0, tiled=True), "expert", axis=1, tiled=True
    )
    mean_all = lax.all_gather(squares / full_width, "tensor", axis=0, tiled=True)
    row_scale = lax.rsqrt(mean_all + epsilon)[:, None]
    experts_local = w_gate.shape[0]
    gate_weight = gate_scores.astype(jnp.float32)
    gate_weight = gate_weight / jnp.sum(gate_weight, axis=1, keepdims=True)
    mixed = None
    for local in range(experts_local):
        expert = lax.axis_index("expert") * experts_local + local
        weight = jnp.sum(jnp.where(expert_ids == expert, gate_weight, 0.0), axis=1, keepdims=True)
        gate_proj = row_scale * lax.dot_general(
            scaled, w_gate[local], (((1,), (1,)), ((), ())), preferred_element_type=jnp.float32
        )
        up_proj = row_scale * lax.dot_general(
            scaled, w_up[local], (((1,), (1,)), ((), ())), preferred_element_type=jnp.float32
        )
        activation = (jax.nn.silu(gate_proj) * up_proj).astype(jnp.bfloat16)
        part = weight * jnp.dot(activation, w_down[local], preferred_element_type=jnp.float32)
        mixed = part if mixed is None else mixed + part
    mixed = lax.psum_scatter(
        mixed.astype(jnp.bfloat16), "tensor", scatter_dimension=0, tiled=True
    )
    mixed_share = lax.psum_scatter(mixed, "expert", scatter_dimension=1, tiled=True)
    return (hidden_state.astype(jnp.bfloat16), mixed_share)


MESH = pl.DeviceIdType.MESH
NZ = 4
UP, DOWN, ACROSS, CORE = 0, 3, 6, 10


def remote(src, dst, send, recv, device):
    return pltpu.make_async_remote_copy(
        src_ref=src, dst_ref=dst, send_sem=send, recv_sem=recv, device_id=device, device_id_type=MESH
    )


class Gather:
    def __init__(self, bufs, sends, recvs, e, y):
        self.bufs, self.sends, self.recvs = bufs, sends, recvs
        self.e, self.y = e, y
        self.z, self.x, self.c = e // 4, (e // 2) % 2, e % 2
        self.ex = e + 2 * (1 - 2 * self.x)
        self.ec = e + 1 - 2 * self.c

    def copies(self, slot, sem, target):
        return [
            remote(
                b.at[slot], b.at[slot], self.sends.at[i, sem], self.recvs.at[i, sem], (target, self.y)
            )
            for i, b in enumerate(self.bufs)
        ]

    def start(self, slot, sem, target):
        for d in self.copies(slot, sem, target):
            d.start()

    def landed(self, slot, sem):
        for d in self.copies(slot, sem, self.ec):
            d.wait_recv()

    def sent(self, slot, sem):
        for d in self.copies(slot, sem, self.ec):
            d.wait_send()

    def slot(self, zz, xx, cc):
        return zz * 4 + xx * 2 + cc

    def forward(self, slot, zz):
        self.start(slot, ACROSS + zz, self.ex)
        self.start(slot, CORE + self.x * NZ + zz, self.ec)

    def run(self):
        z, x, c, e = self.z, self.x, self.c, self.e

        @pl.when(z < NZ - 1)
        def _():
            self.start(e, UP, e + 4)

        @pl.when(z > 0)
        def _():
            self.start(e, DOWN, e - 4)

        self.forward(e, z)
        for k in range(1, NZ):

            @pl.when(z - k >= 0)
            def _(k=k):
                slot = e - 4 * k
                self.landed(slot, UP + k - 1)
                if k < NZ - 1:

                    @pl.when(z < NZ - 1)
                    def _():
                        self.start(slot, UP + k, e + 4)

                self.forward(slot, z - k)

            @pl.when(z + k <= NZ - 1)
            def _(k=k):
                slot = e + 4 * k
                self.landed(slot, DOWN + k - 1)
                if k < NZ - 1:

                    @pl.when(z > 0)
                    def _():
                        self.start(slot, DOWN + k, e - 4)

                self.forward(slot, z + k)

        step = 1 - 2 * (z // 2)
        for j in range(NZ):
            zz = (z + step * j + NZ) % NZ
            slot = self.slot(zz, 1 - x, c)
            self.landed(slot, ACROSS + zz)
            self.start(slot, CORE + (1 - x) * NZ + zz, self.ec)

    def wait_core(self):
        for xx in range(2):
            for zz in range(NZ):
                self.landed(self.slot(zz, xx, 1 - self.c), CORE + xx * NZ + zz)

    def wait_sends(self):
        z, e = self.z, self.e
        for k in range(1, NZ):

            @pl.when((z < NZ - 1) & (z - (k - 1) >= 0))
            def _(k=k):
                self.sent(e - 4 * (k - 1), UP + k - 1)

            @pl.when((z > 0) & (z + k - 1 <= NZ - 1))
            def _(k=k):
                self.sent(e + 4 * (k - 1), DOWN + k - 1)

        for zz in range(NZ):
            self.sent(self.slot(zz, self.x, self.c), ACROSS + zz)
            for xx in range(2):
                self.sent(self.slot(zz, xx, self.c), CORE + xx * NZ + zz)


def nt_dot(a, b):
    return lax.dot_general(a, b, (((1,), (1,)), ((), ())), preferred_element_type=jnp.float32)


def layer_kernel(
    q_ref, k_hbm, v_hbm, len_ref, res_ref, wo_hbm, gain_ref, ids_ref, gates_ref,
    wg_hbm, wu_hbm, wd_hbm,
    hid_ref, mix_ref,
    k_v, v_v, wo_v, wg_v, wu_v, wd_v, local_sems,
    lay, qlay, sblk, ctx, part, part_in, hid_all, sq_all,
    gate_acc, up_acc, act, own, tmp, core_in, xout, x_in, zout, up_in, down_in, yout, y_in,
    c_send, c_recv, h_send, h_recv, p_send, p_recv, r_send, r_recv,
):
    f32, bf16 = jnp.float32, jnp.bfloat16
    e = lax.axis_index("expert")
    y = lax.axis_index("tensor")
    z, x, c = e // 4, (e // 2) % 2, e % 2
    ex, ec = e + 2 * (1 - 2 * x), e + 1 - 2 * c
    barrier = pltpu.get_barrier_semaphore()
    pairs = [(k_hbm, k_v), (v_hbm, v_v), (wo_hbm, wo_v), (wg_hbm, wg_v), (wu_hbm, wu_v), (wd_hbm, wd_v)]
    loads = [pltpu.make_async_copy(s, d, local_sems.at[i]) for i, (s, d) in enumerate(pairs)]
    for d in loads:
        d.start()
    for dev in ((ec, y), (ex, y), (e, 1 - y)):
        pl.semaphore_signal(barrier, inc=1, device_id=dev, device_id_type=MESH)

    @pl.when(z > 0)
    def _():
        pl.semaphore_signal(barrier, inc=1, device_id=(e - 4, y), device_id_type=MESH)

    @pl.when(z < NZ - 1)
    def _():
        pl.semaphore_signal(barrier, inc=1, device_id=(e + 4, y), device_id_type=MESH)

    rows = q_ref.shape[0]
    for h in range(64):
        qlay[h * 8 : h * 8 + rows, :] = q_ref[:, h * 128 : (h + 1) * 128].astype(f32)
    loads[0].wait()
    loads[1].wait()
    col = lax.broadcasted_iota(jnp.int32, (64, 512), 1)
    head = lax.broadcasted_iota(jnp.int32, (64, 512), 0)
    same = (col % 4) == (head // 16)
    for r in range(rows):
        q = qlay[pl.ds(r, 64, stride=8), :].astype(bf16)
        s = nt_dot(q, k_v[r]) * (128 ** -0.5)
        ok = same & ((col // 4) < len_ref[r])
        peak = jnp.max(jnp.where(ok, s, -1e30), axis=1, keepdims=True)
        w = jnp.where(ok, jnp.exp(s - peak), 0.0)
        total = jnp.sum(w, axis=1, keepdims=True)
        o = jnp.dot(w.astype(bf16), v_v[r], preferred_element_type=f32) / total
        for half in range(2):
            for j in range(4):
                h0 = half * 32 + j * 8
                lay[pl.ds(half * 128 + 4 * j + r, 8, stride=16), :] = o[h0 : h0 + 8]
    for half in range(2):
        for hh in range(8):
            t = (half * 8 + hh) * 16
            sblk[half, :, hh * 128 : (hh + 1) * 128] = lay[t : t + 16, :].astype(bf16)
    ctx[e, y] = sblk[y]
    pl.semaphore_wait(barrier, 4 + z * (NZ - 1 - z) // 2)

    swap = remote(sblk.at[1 - y], ctx.at[e, y], p_send.at[0], p_recv.at[0], (e, 1 - y))
    swap.start()
    swap.wait_recv()
    g1 = Gather([ctx], c_send, c_recv, e, y)
    g1.run()
    g1.wait_core()

    loads[2].wait()
    lhs = ctx.reshape(512, 1024)
    quarter = (lax.broadcasted_iota(jnp.int32, (512, 256), 0) % 16) // 4
    acc = jnp.zeros((512, 256), f32)
    for j in range(4):
        pj = nt_dot(lhs[...], wo_v[:, j * 1024 : (j + 1) * 1024])
        acc = jnp.where(quarter == j, pj, acc)
    folded = acc.reshape(32, 2, 8, 256)
    folded = (folded[:, 0] + folded[:, 1]).reshape(256, 256)
    low = (lax.broadcasted_iota(jnp.int32, (256, 256), 0) % 8) < 4
    folded = folded + jnp.where(low, pltpu.roll(folded, 252, 0), pltpu.roll(folded, 4, 0))
    folded = folded.reshape(16, 2, 8, 256)
    low3 = lax.broadcasted_iota(jnp.int32, (16, 8, 256), 1) < 4
    part[...] = jnp.where(low3, folded[:, 0], folded[:, 1]).reshape(2, 64, 256)
    psend = remote(part.at[1 - y], part_in, p_send.at[1], p_recv.at[1], (e, 1 - y))
    psend.start()
    psend.wait_recv()
    hidden = res_ref[...].astype(f32) + (part[y] + part_in[...])
    hid_ref[...] = hidden.astype(bf16)
    hid_all[e, y] = (hidden * gain_ref[...].astype(f32)).astype(bf16)
    ss = jnp.sum(hidden * hidden, axis=1, keepdims=True)
    place = lax.broadcasted_iota(jnp.int32, (64, 128), 0) + 64 * y
    lane = lax.broadcasted_iota(jnp.int32, (64, 128), 1)
    sq = jnp.sum(jnp.where(place == lane, ss, 0.0), axis=0, keepdims=True)
    sq_all[e, y] = jnp.broadcast_to(sq, (8, 128))
    hs = remote(hid_all.at[e, y], hid_all.at[e, y], p_send.at[2], p_recv.at[2], (e, 1 - y))
    qs = remote(sq_all.at[e, y], sq_all.at[e, y], p_send.at[3], p_recv.at[3], (e, 1 - y))
    hs.start()
    qs.start()
    hs.wait_recv()
    qs.wait_recv()
    g2 = Gather([hid_all, sq_all], h_send, h_recv, e, y)
    g2.run()
    loads[3].wait()
    loads[4].wait()

    def products(core, first):
        def step(n, _):
            rows_n = pl.ds(pl.multiple_of(n * 256, 256), 256)
            for wref, aref in ((wg_v, gate_acc), (wu_v, up_acc)):
                a = jnp.zeros((128, 256), f32) if first else aref[n]
                for j in range(8):
                    src = 2 * j + core
                    cols = pl.ds(pl.multiple_of(src * 256, 256), 256)
                    a = a + nt_dot(hid_all[src].reshape(128, 256), wref[rows_n, cols])
                aref[n] = a
            return 0

        lax.fori_loop(0, 3, step, 0)

    products(c, True)
    g2.wait_core()
    products(1 - c, False)
    total = jnp.sum(sq_all[...].reshape(32, 8, 128), axis=0)
    scale_row = lax.rsqrt(total[0:1] / 4096.0 + epsilon)
    eye = lax.broadcasted_iota(jnp.int32, (128, 128), 0) == lax.broadcasted_iota(jnp.int32, (128, 128), 1)
    scale = jnp.sum(jnp.where(eye, scale_row, 0.0), axis=1, keepdims=True)
    gw = gates_ref[...].astype(f32)
    gw = gw / jnp.sum(gw, axis=1, keepdims=True)
    weight = jnp.sum(jnp.where(ids_ref[...] == e, gw, 0.0), axis=1, keepdims=True)
    for n in range(3):
        g = gate_acc[n] * scale
        u = up_acc[n] * scale
        act[:, n * 256 : (n + 1) * 256] = (g / (1.0 + jnp.exp(-g)) * u).astype(bf16)
    loads[5].wait()

    def block(zz, xx, cc):
        cols = pl.ds(pl.multiple_of((zz * 4 + xx * 2 + cc) * 256, 256), 256)
        return jnp.dot(act[...], wd_v[:, cols], preferred_element_type=f32) * weight

    def core_copy(b):
        return remote(tmp.at[b], core_in.at[b], r_send.at[b], r_recv.at[b], (ec, y))

    def x_copy(b):
        return remote(xout.at[b], x_in.at[b], r_send.at[8 + b], r_recv.at[8 + b], (ex, y))

    def other_core(i, _):
        xx = (1 - x + i // 4) % 2
        b = xx * 4 + i % 4
        tmp[b] = block(i % 4, xx, 1 - c).astype(bf16)
        core_copy(b).start()
        return 0

    lax.fori_loop(0, 8, other_core, 0)

    def far(zz, _):
        p = block(zz, 1 - x, c)
        b = (1 - x) * 4 + zz
        core_copy(b).wait_recv()
        xout[zz] = (p + core_in[b].astype(f32)).astype(bf16)
        x_copy(zz).start()
        return 0

    lax.fori_loop(0, 4, far, 0)

    def near(zz, _):
        p = block(zz, x, c)
        b = x * 4 + zz
        core_copy(b).wait_recv()
        own[zz] = p + core_in[b].astype(f32)
        return 0

    lax.fori_loop(0, 4, near, 0)

    def x_done(zz, _):
        x_copy(zz).wait_recv()
        own[zz] = own[zz] + x_in[zz].astype(f32)
        return 0

    lax.fori_loop(0, 4, x_done, 0)

    def up_copy(zz):
        return remote(zout.at[zz], up_in.at[zz], r_send.at[12 + zz], r_recv.at[12 + zz], (e + 4, y))

    def down_copy(zz):
        return remote(zout.at[zz], down_in.at[zz], r_send.at[12 + zz], r_recv.at[16 + zz], (e - 4, y))

    for k in range(NZ - 1, 0, -1):

        @pl.when(z + k <= NZ - 1)
        def _(k=k):
            zz = z + k

            @pl.when(z > 0)
            def _():
                up_copy(zz).wait_recv()
                own[zz] = own[zz] + up_in[zz].astype(f32)

            zout[zz] = own[zz].astype(bf16)
            up_copy(zz).start()

        @pl.when(z - k >= 0)
        def _(k=k):
            zz = z - k

            @pl.when(z < NZ - 1)
            def _():
                down_copy(zz).wait_recv()
                own[zz] = own[zz] + down_in[zz].astype(f32)

            zout[zz] = own[zz].astype(bf16)
            down_copy(zz).start()

    @pl.when(z > 0)
    def _():
        up_copy(z).wait_recv()
        own[z] = own[z] + up_in[z].astype(f32)

    @pl.when(z < NZ - 1)
    def _():
        down_copy(z).wait_recv()
        own[z] = own[z] + down_in[z].astype(f32)

    final = own.at[z].reshape(2, 64, 256)
    yout[...] = final[1 - y].astype(bf16)
    ysend = remote(yout, y_in, p_send.at[4], p_recv.at[4], (e, 1 - y))
    ysend.start()
    ysend.wait_recv()
    mix_ref[...] = (final[y] + y_in[...].astype(f32)).astype(bf16)

    for d in (swap, psend, hs, qs, ysend):
        d.wait_send()
    g1.wait_sends()
    g2.wait_sends()
    for b in range(8):
        core_copy(b).wait_send()
    for b in range(4):
        x_copy(b).wait_send()
    for k in range(1, NZ):

        @pl.when(z + k <= NZ - 1)
        def _(k=k):
            up_copy(z + k).wait_send()

        @pl.when(z - k >= 0)
        def _(k=k):
            down_copy(z - k).wait_send()


def fused_body(
    query, cache_keys, cache_values, lengths, residual, out_proj, norm_gain, expert_ids, gate_scores,
    w_gate, w_up, w_down,
):
    f32, bf16 = jnp.float32, jnp.bfloat16
    rows = query.shape[0]
    keys = cache_keys.reshape(rows, 512, 128)
    values = cache_values.reshape(rows, 512, 128)
    vm = pl.BlockSpec(memory_space=pltpu.VMEM)
    hb = pl.BlockSpec(memory_space=pl.ANY)
    sm = pl.BlockSpec(memory_space=pltpu.SMEM)
    V, S = pltpu.VMEM, pltpu.SemaphoreType.DMA
    return pl.pallas_call(
        layer_kernel,
        name="layer",
        out_shape=(jax.ShapeDtypeStruct((64, 256), bf16), jax.ShapeDtypeStruct((64, 256), bf16)),
        in_specs=[vm, hb, hb, sm, vm, hb, vm, vm, vm, hb, hb, hb],
        out_specs=(vm, vm),
        scratch_shapes=[
            V((rows, 512, 128), bf16), V((rows, 512, 128), bf16), V((256, 4096), bf16),
            V((768, 4096), bf16), V((768, 4096), bf16), V((768, 4096), bf16), S((6,)),
            V((256, 128), f32), V((512, 128), f32), V((2, 16, 1024), bf16), V((16, 2, 16, 1024), bf16),
            V((2, 64, 256), f32), V((64, 256), f32), V((16, 2, 64, 256), bf16), V((16, 2, 8, 128), f32),
            V((3, 128, 256), f32), V((3, 128, 256), f32), V((128, 768), bf16),
            V((4, 128, 256), f32), V((8, 128, 256), bf16), V((8, 128, 256), bf16),
            V((4, 128, 256), bf16), V((4, 128, 256), bf16), V((4, 128, 256), bf16),
            V((4, 128, 256), bf16), V((4, 128, 256), bf16), V((64, 256), bf16), V((64, 256), bf16),
            S((1, 18)), S((1, 18)), S((2, 18)), S((2, 18)), S((5,)), S((5,)), S((20,)), S((20,)),
        ],
        compiler_params=pltpu.CompilerParams(
            collective_id=0, has_side_effects=True, vmem_limit_bytes=62 * 1024 * 1024
        ),
    )(
        query, keys, values, lengths, residual, out_proj, norm_gain.reshape(1, -1), expert_ids,
        gate_scores, w_gate[0], w_up[0], w_down[0],
    )


def solution(mesh):
    in_specs = (
        P(("expert", "tensor"), None),
        P(("expert", "tensor"), None, None, None),
        P(("expert", "tensor"), None, None, None),
        P(("expert", "tensor")),
        P("tensor", "expert"),
        P("expert", "tensor"),
        P("expert"),
        P(),
        P(),
        P("expert", "tensor", None),
        P("expert", "tensor", None),
        P("expert", "tensor", None),
    )
    out_specs = (P("tensor", "expert"), P("tensor", "expert"))
    fused = dict(mesh.shape) == {"expert": 16, "tensor": 2}
    return jax.shard_map(fused_body if fused else body, mesh=mesh, in_specs=in_specs, out_specs=out_specs, check_vma=False)
```

```python
import jax
import jax.numpy as jnp
from jax import lax
from jax.experimental import pallas as pl
from jax.experimental.pallas import tpu as pltpu
from jax.sharding import PartitionSpec as P

floor_value = -1e30
epsilon = 1e-06


def softmax_parts(queries, key_block, value_block, usable, score_scale):
    scores = (
        jnp.einsum("rkgd,rpkd->rkgp", queries, key_block, preferred_element_type=jnp.float32)
        * score_scale
    )
    usable_mask = usable[:, None, None, :]
    peak = jnp.max(jnp.where(usable_mask, scores, floor_value), axis=-1)
    raw_weights = jnp.where(usable_mask, jnp.exp(scores - peak[..., None]), 0.0)
    weight_sum = jnp.sum(raw_weights, axis=-1)
    weighted = jnp.einsum("rkgp,rpkd->rkgd", raw_weights, value_block.astype(jnp.float32))
    return (weight_sum, weighted)


def body(
    query,
    cache_keys,
    cache_values,
    lengths,
    residual,
    out_proj,
    norm_gain,
    expert_ids,
    gate_scores,
    w_gate,
    w_up,
    w_down,
):
    row_count, full_heads_width = query.shape
    cache_len = cache_keys.shape[1]
    kv_count = cache_keys.shape[2]
    head_size = cache_keys.shape[3]
    head_count = full_heads_width // head_size
    group_size = head_count // kv_count
    score_scale = head_size ** (-0.5)
    usable = jnp.arange(cache_len, dtype=jnp.int32)[None, :] < lengths[:, None]
    grouped = query.reshape(row_count, kv_count, group_size, head_size)
    weight_sum, weighted = softmax_parts(grouped, cache_keys, cache_values, usable, score_scale)
    context_rows_own = (
        (weighted / weight_sum[..., None]).astype(jnp.bfloat16).reshape(row_count, full_heads_width)
    )
    context = lax.all_to_all(context_rows_own, "tensor", split_axis=1, concat_axis=0, tiled=True)
    attn_part = jnp.dot(
        lax.all_gather(context, "expert", axis=0, tiled=True),
        out_proj.T,
        preferred_element_type=jnp.float32,
    )
    attn_share = lax.psum_scatter(attn_part, "tensor", scatter_dimension=0, tiled=True)
    hidden_state = residual.astype(jnp.float32) + attn_share
    squares = lax.psum(jnp.sum(hidden_state * hidden_state, axis=1), "expert")
    full_width = hidden_state.shape[1] * lax.axis_size("expert")
    scaled_share = (hidden_state * norm_gain.astype(jnp.float32)[None, :]).astype(jnp.bfloat16)
    scaled = lax.all_gather(
        lax.all_gather(scaled_share, "tensor", axis=0, tiled=True), "expert", axis=1, tiled=True
    )
    mean_all = lax.all_gather(squares / full_width, "tensor", axis=0, tiled=True)
    row_scale = lax.rsqrt(mean_all + epsilon)[:, None]
    experts_local = w_gate.shape[0]
    gate_weight = gate_scores.astype(jnp.float32)
    gate_weight = gate_weight / jnp.sum(gate_weight, axis=1, keepdims=True)
    mixed = None
    for local in range(experts_local):
        expert = lax.axis_index("expert") * experts_local + local
        weight = jnp.sum(jnp.where(expert_ids == expert, gate_weight, 0.0), axis=1, keepdims=True)
        gate_proj = row_scale * lax.dot_general(
            scaled, w_gate[local], (((1,), (1,)), ((), ())), preferred_element_type=jnp.float32
        )
        up_proj = row_scale * lax.dot_general(
            scaled, w_up[local], (((1,), (1,)), ((), ())), preferred_element_type=jnp.float32
        )
        activation = (jax.nn.silu(gate_proj) * up_proj).astype(jnp.bfloat16)
        part = weight * jnp.dot(activation, w_down[local], preferred_element_type=jnp.float32)
        mixed = part if mixed is None else mixed + part
    mixed = lax.psum_scatter(
        mixed.astype(jnp.bfloat16), "tensor", scatter_dimension=0, tiled=True
    )
    mixed_share = lax.psum_scatter(mixed, "expert", scatter_dimension=1, tiled=True)
    return (hidden_state.astype(jnp.bfloat16), mixed_share)


MESH = pl.DeviceIdType.MESH
NZ = 4
UP, DOWN, ACROSS, CORE = 0, 3, 6, 10


def remote(src, dst, send, recv, device):
    return pltpu.make_async_remote_copy(
        src_ref=src, dst_ref=dst, send_sem=send, recv_sem=recv, device_id=device, device_id_type=MESH
    )


class Gather:
    def __init__(self, bufs, sends, recvs, e, y):
        self.bufs, self.sends, self.recvs = bufs, sends, recvs
        self.e, self.y = e, y
        self.z, self.x, self.c = e // 4, (e // 2) % 2, e % 2
        self.ex = e + 2 * (1 - 2 * self.x)
        self.ec = e + 1 - 2 * self.c

    def copies(self, slot, sem, target):
        return [
            remote(
                b.at[slot], b.at[slot], self.sends.at[i, sem], self.recvs.at[i, sem], (target, self.y)
            )
            for i, b in enumerate(self.bufs)
        ]

    def start(self, slot, sem, target):
        for d in self.copies(slot, sem, target):
            d.start()

    def landed(self, slot, sem):
        for d in self.copies(slot, sem, self.ec):
            d.wait_recv()

    def sent(self, slot, sem):
        for d in self.copies(slot, sem, self.ec):
            d.wait_send()

    def slot(self, zz, xx, cc):
        return zz * 4 + xx * 2 + cc

    def forward(self, slot, zz):
        self.start(slot, ACROSS + zz, self.ex)
        self.start(slot, CORE + self.x * NZ + zz, self.ec)

    def run(self):
        z, x, c, e = self.z, self.x, self.c, self.e

        @pl.when(z < NZ - 1)
        def _():
            self.start(e, UP, e + 4)

        @pl.when(z > 0)
        def _():
            self.start(e, DOWN, e - 4)

        self.forward(e, z)
        for k in range(1, NZ):

            @pl.when(z - k >= 0)
            def _(k=k):
                slot = e - 4 * k
                self.landed(slot, UP + k - 1)
                if k < NZ - 1:

                    @pl.when(z < NZ - 1)
                    def _():
                        self.start(slot, UP + k, e + 4)

                self.forward(slot, z - k)

            @pl.when(z + k <= NZ - 1)
            def _(k=k):
                slot = e + 4 * k
                self.landed(slot, DOWN + k - 1)
                if k < NZ - 1:

                    @pl.when(z > 0)
                    def _():
                        self.start(slot, DOWN + k, e - 4)

                self.forward(slot, z + k)

        step = 1 - 2 * (z // 2)
        for j in range(NZ):
            zz = (z + step * j + NZ) % NZ
            slot = self.slot(zz, 1 - x, c)
            self.landed(slot, ACROSS + zz)
            self.start(slot, CORE + (1 - x) * NZ + zz, self.ec)

    def wait_core(self):
        for xx in range(2):
            for zz in range(NZ):
                self.landed(self.slot(zz, xx, 1 - self.c), CORE + xx * NZ + zz)

    def wait_sends(self):
        z, e = self.z, self.e
        for k in range(1, NZ):

            @pl.when((z < NZ - 1) & (z - (k - 1) >= 0))
            def _(k=k):
                self.sent(e - 4 * (k - 1), UP + k - 1)

            @pl.when((z > 0) & (z + k - 1 <= NZ - 1))
            def _(k=k):
                self.sent(e + 4 * (k - 1), DOWN + k - 1)

        for zz in range(NZ):
            self.sent(self.slot(zz, self.x, self.c), ACROSS + zz)
            for xx in range(2):
                self.sent(self.slot(zz, xx, self.c), CORE + xx * NZ + zz)


def nt_dot(a, b):
    return lax.dot_general(a, b, (((1,), (1,)), ((), ())), preferred_element_type=jnp.float32)


def layer_kernel(
    q_ref, k_hbm, v_hbm, len_ref, res_ref, wo_hbm, gain_ref, ids_ref, gates_ref,
    wg_hbm, wu_hbm, wd_hbm,
    hid_ref, mix_ref,
    k_v, v_v, wo_v, wg_v, wu_v, wd_v, local_sems,
    lay, qlay, sblk, ctx, part, part_in, hid_all, sq_all,
    gate_acc, up_acc, act, own, fin, tmp, core_in, y0_out, y0_in, x1_out, x1_in, x0_out, x0_in,
    y1_out, y1_in, zout, up_in, down_in,
    c_send, c_recv, h_send, h_recv, p_send, p_recv, r_send, r_recv,
):
    f32, bf16 = jnp.float32, jnp.bfloat16
    e = lax.axis_index("expert")
    y = lax.axis_index("tensor")
    z, x, c = e // 4, (e // 2) % 2, e % 2
    ex, ec = e + 2 * (1 - 2 * x), e + 1 - 2 * c
    barrier = pltpu.get_barrier_semaphore()
    pairs = [(k_hbm, k_v), (v_hbm, v_v), (wo_hbm, wo_v), (wg_hbm, wg_v), (wu_hbm, wu_v), (wd_hbm, wd_v)]
    loads = [pltpu.make_async_copy(s, d, local_sems.at[i]) for i, (s, d) in enumerate(pairs)]
    loads[0].start()
    loads[1].start()
    for dev in ((ec, y), (ex, y), (e, 1 - y)):
        pl.semaphore_signal(barrier, inc=1, device_id=dev, device_id_type=MESH)

    @pl.when(z > 0)
    def _():
        pl.semaphore_signal(barrier, inc=1, device_id=(e - 4, y), device_id_type=MESH)

    @pl.when(z < NZ - 1)
    def _():
        pl.semaphore_signal(barrier, inc=1, device_id=(e + 4, y), device_id_type=MESH)

    rows = q_ref.shape[0]
    for h in range(64):
        qlay[h * 8 : h * 8 + rows, :] = q_ref[:, h * 128 : (h + 1) * 128].astype(f32)
    loads[0].wait()
    loads[1].wait()
    for d in loads[2:]:
        d.start()
    col = lax.broadcasted_iota(jnp.int32, (64, 512), 1)
    head = lax.broadcasted_iota(jnp.int32, (64, 512), 0)
    same = (col % 4) == (head // 16)
    for r in range(rows):
        q = qlay[pl.ds(r, 64, stride=8), :].astype(bf16)
        s = nt_dot(q, k_v[r]) * (128 ** -0.5)
        ok = same & ((col // 4) < len_ref[r])
        peak = jnp.max(jnp.where(ok, s, -1e30), axis=1, keepdims=True)
        w = jnp.where(ok, jnp.exp(s - peak), 0.0)
        total = jnp.sum(w, axis=1, keepdims=True)
        o = jnp.dot(w.astype(bf16), v_v[r], preferred_element_type=f32) / total
        for half in range(2):
            for j in range(4):
                h0 = half * 32 + j * 8
                lay[pl.ds(half * 128 + 4 * j + r, 8, stride=16), :] = o[h0 : h0 + 8]
    for half in range(2):
        for hh in range(8):
            t = (half * 8 + hh) * 16
            sblk[half, :, hh * 128 : (hh + 1) * 128] = lay[t : t + 16, :].astype(bf16)
    ctx[e, y] = sblk[y]
    pl.semaphore_wait(barrier, 4 + z * (NZ - 1 - z) // 2)

    swap = remote(sblk.at[1 - y], ctx.at[e, y], p_send.at[0], p_recv.at[0], (e, 1 - y))
    swap.start()
    swap.wait_recv()
    g1 = Gather([ctx], c_send, c_recv, e, y)
    g1.run()
    g1.wait_core()

    loads[2].wait()
    lhs = ctx.reshape(512, 1024)
    quarter = (lax.broadcasted_iota(jnp.int32, (512, 256), 0) % 16) // 4
    acc = jnp.zeros((512, 256), f32)
    for j in range(4):
        pj = nt_dot(lhs[...], wo_v[:, j * 1024 : (j + 1) * 1024])
        acc = jnp.where(quarter == j, pj, acc)
    folded = acc.reshape(32, 2, 8, 256)
    folded = (folded[:, 0] + folded[:, 1]).reshape(256, 256)
    low = (lax.broadcasted_iota(jnp.int32, (256, 256), 0) % 8) < 4
    folded = folded + jnp.where(low, pltpu.roll(folded, 252, 0), pltpu.roll(folded, 4, 0))
    folded = folded.reshape(16, 2, 8, 256)
    low3 = lax.broadcasted_iota(jnp.int32, (16, 8, 256), 1) < 4
    part[...] = jnp.where(low3, folded[:, 0], folded[:, 1]).reshape(2, 64, 256)
    psend = remote(part.at[1 - y], part_in, p_send.at[1], p_recv.at[1], (e, 1 - y))
    psend.start()
    psend.wait_recv()
    hidden = res_ref[...].astype(f32) + (part[y] + part_in[...])
    hid_ref[...] = hidden.astype(bf16)
    hid_all[e, y] = (hidden * gain_ref[...].astype(f32)).astype(bf16)
    ss = jnp.sum(hidden * hidden, axis=1, keepdims=True)
    place = lax.broadcasted_iota(jnp.int32, (64, 128), 0) + 64 * y
    lane = lax.broadcasted_iota(jnp.int32, (64, 128), 1)
    sq = jnp.sum(jnp.where(place == lane, ss, 0.0), axis=0, keepdims=True)
    sq_all[e, y] = jnp.broadcast_to(sq, (8, 128))
    hs = remote(hid_all.at[e, y], hid_all.at[e, y], p_send.at[2], p_recv.at[2], (e, 1 - y))
    qs = remote(sq_all.at[e, y], sq_all.at[e, y], p_send.at[3], p_recv.at[3], (e, 1 - y))
    hs.start()
    qs.start()
    hs.wait_recv()
    qs.wait_recv()
    g2 = Gather([hid_all, sq_all], h_send, h_recv, e, y)
    g2.run()
    loads[3].wait()
    loads[4].wait()

    def products(core, first):
        def step(n, _):
            rows_n = pl.ds(pl.multiple_of(n * 256, 256), 256)
            for wref, aref in ((wg_v, gate_acc), (wu_v, up_acc)):
                a = jnp.zeros((128, 256), f32) if first else aref[n]
                for j in range(8):
                    src = 2 * j + core
                    cols = pl.ds(pl.multiple_of(src * 256, 256), 256)
                    a = a + nt_dot(hid_all[src].reshape(128, 256), wref[rows_n, cols])
                aref[n] = a
            return 0

        lax.fori_loop(0, 3, step, 0)

    products(c, True)
    g2.wait_core()
    products(1 - c, False)
    total = jnp.sum(sq_all[...].reshape(32, 8, 128), axis=0)
    scale_row = lax.rsqrt(total[0:1] / 4096.0 + epsilon)
    eye = lax.broadcasted_iota(jnp.int32, (128, 128), 0) == lax.broadcasted_iota(jnp.int32, (128, 128), 1)
    scale = jnp.sum(jnp.where(eye, scale_row, 0.0), axis=1, keepdims=True)
    gw = gates_ref[...].astype(f32)
    gw = gw / jnp.sum(gw, axis=1, keepdims=True)
    weight = jnp.sum(jnp.where(ids_ref[...] == e, gw, 0.0), axis=1, keepdims=True)
    for n in range(3):
        g = gate_acc[n] * scale
        u = up_acc[n] * scale
        act[:, n * 256 : (n + 1) * 256] = (g / (1.0 + jnp.exp(-g)) * u).astype(bf16)
    loads[5].wait()

    def block(zz, xx, cc):
        cols = pl.ds(pl.multiple_of((zz * 4 + xx * 2 + cc) * 256, 256), 256)
        p = jnp.dot(act[...], wd_v[:, cols], preferred_element_type=f32) * weight
        return p.reshape(2, 2, 32, 256)

    mirror = z // 2
    near_z = z + mirror * (3 - 2 * z)

    def far_first(i):
        o = (3, 2, 1 - near_z, near_z)[i]
        return o + mirror * (3 - 2 * o)

    def core_copy(b):
        return remote(tmp.at[b], core_in.at[b], r_send.at[b], r_recv.at[b], (ec, y))

    def y0_copy(b):
        return remote(y0_out.at[b], y0_in.at[b], r_send.at[8 + b], r_recv.at[8 + b], (e, 1 - y))

    def x1_copy(zz):
        return remote(x1_out.at[zz], x1_in.at[zz], r_send.at[16 + zz], r_recv.at[16 + zz], (ex, y))

    def x0_copy(zz):
        return remote(x0_out.at[zz], x0_in.at[zz], r_send.at[20 + zz], r_recv.at[20 + zz], (ex, y))

    def y1_copy(zz):
        return remote(y1_out.at[zz], y1_in.at[zz], r_send.at[24 + zz], r_recv.at[24 + zz], (e, 1 - y))

    def up_copy(zz):
        return remote(zout.at[zz], up_in.at[zz], r_send.at[28 + zz], r_recv.at[28 + zz], (e + 4, y))

    def down_copy(zz):
        return remote(zout.at[zz], down_in.at[zz], r_send.at[28 + zz], r_recv.at[32 + zz], (e - 4, y))

    for i in range(NZ):
        zz = far_first(i)
        for xx in (1 - x, x):
            b = xx * 4 + zz
            tmp[b] = block(zz, xx, 1 - c).astype(bf16)
            core_copy(b).start()

    for i in range(NZ):
        zz = far_first(i)
        for n, xx in enumerate((1 - x, x)):
            b = xx * 4 + zz
            own[b] = block(zz, xx, c)
            core_copy(b).wait_recv()
            own[b] = own[b] + core_in[b].astype(f32)
            y0_out[b] = own[b, 1 - y, 0].astype(bf16)
            y0_copy(b).start()
            if n == 0:
                x1_out[zz] = own[b, :, 1].astype(bf16)
                x1_copy(zz).start()

    for i in range(NZ):
        zz = far_first(i)
        far, near = (1 - x) * 4 + zz, x * 4 + zz
        x1_copy(zz).wait_recv()
        y1_out[zz] = (own[near, 1 - y, 1] + x1_in[zz, 1 - y].astype(f32)).astype(bf16)
        y1_copy(zz).start()
        y0_copy(far).wait_recv()
        x0_out[zz] = (own[far, y, 0] + y0_in[far].astype(f32)).astype(bf16)
        x0_copy(zz).start()

    for i in range(NZ):
        zz = far_first(i)
        near = x * 4 + zz
        y0_copy(near).wait_recv()
        x0_copy(zz).wait_recv()
        y1_copy(zz).wait_recv()
        fin[zz, 0] = own[near, y, 0] + y0_in[near].astype(f32) + x0_in[zz].astype(f32)
        fin[zz, 1] = own[near, y, 1] + x1_in[zz, y].astype(f32) + y1_in[zz].astype(f32)

        if i < NZ - 1:

            @pl.when(zz > z)
            def _():
                @pl.when(z > 0)
                def _():
                    up_copy(zz).wait_recv()
                    fin[zz] = fin[zz] + up_in[zz].astype(f32)

                zout[zz] = fin[zz].astype(bf16)
                up_copy(zz).start()

            @pl.when(zz < z)
            def _():
                @pl.when(z < NZ - 1)
                def _():
                    down_copy(zz).wait_recv()
                    fin[zz] = fin[zz] + down_in[zz].astype(f32)

                zout[zz] = fin[zz].astype(bf16)
                down_copy(zz).start()

    @pl.when(z > 0)
    def _():
        up_copy(z).wait_recv()
        fin[z] = fin[z] + up_in[z].astype(f32)

    @pl.when(z < NZ - 1)
    def _():
        down_copy(z).wait_recv()
        fin[z] = fin[z] + down_in[z].astype(f32)

    mix_ref[...] = fin[z].reshape(64, 256).astype(bf16)

    for d in (swap, psend, hs, qs):
        d.wait_send()
    g1.wait_sends()
    g2.wait_sends()
    for b in range(8):
        core_copy(b).wait_send()
        y0_copy(b).wait_send()
    for zz in range(NZ):
        x1_copy(zz).wait_send()
        x0_copy(zz).wait_send()
        y1_copy(zz).wait_send()
    for k in range(1, NZ):

        @pl.when(z + k <= NZ - 1)
        def _(k=k):
            up_copy(z + k).wait_send()

        @pl.when(z - k >= 0)
        def _(k=k):
            down_copy(z - k).wait_send()


def fused_body(
    query, cache_keys, cache_values, lengths, residual, out_proj, norm_gain, expert_ids, gate_scores,
    w_gate, w_up, w_down,
):
    f32, bf16 = jnp.float32, jnp.bfloat16
    rows = query.shape[0]
    keys = cache_keys.reshape(rows, 512, 128)
    values = cache_values.reshape(rows, 512, 128)
    vm = pl.BlockSpec(memory_space=pltpu.VMEM)
    hb = pl.BlockSpec(memory_space=pl.ANY)
    sm = pl.BlockSpec(memory_space=pltpu.SMEM)
    V, S = pltpu.VMEM, pltpu.SemaphoreType.DMA
    return pl.pallas_call(
        layer_kernel,
        name="layer",
        out_shape=(jax.ShapeDtypeStruct((64, 256), bf16), jax.ShapeDtypeStruct((64, 256), bf16)),
        in_specs=[vm, hb, hb, sm, vm, hb, vm, vm, vm, hb, hb, hb],
        out_specs=(vm, vm),
        scratch_shapes=[
            V((rows, 512, 128), bf16), V((rows, 512, 128), bf16), V((256, 4096), bf16),
            V((768, 4096), bf16), V((768, 4096), bf16), V((768, 4096), bf16), S((6,)),
            V((256, 128), f32), V((512, 128), f32), V((2, 16, 1024), bf16), V((16, 2, 16, 1024), bf16),
            V((2, 64, 256), f32), V((64, 256), f32), V((16, 2, 64, 256), bf16), V((16, 2, 8, 128), f32),
            V((3, 128, 256), f32), V((3, 128, 256), f32), V((128, 768), bf16),
            V((8, 2, 2, 32, 256), f32), V((4, 2, 32, 256), f32),
            V((8, 2, 2, 32, 256), bf16), V((8, 2, 2, 32, 256), bf16),
            V((8, 32, 256), bf16), V((8, 32, 256), bf16),
            V((4, 2, 32, 256), bf16), V((4, 2, 32, 256), bf16),
            V((4, 32, 256), bf16), V((4, 32, 256), bf16),
            V((4, 32, 256), bf16), V((4, 32, 256), bf16),
            V((4, 2, 32, 256), bf16), V((4, 2, 32, 256), bf16), V((4, 2, 32, 256), bf16),
            S((1, 18)), S((1, 18)), S((2, 18)), S((2, 18)), S((4,)), S((4,)), S((36,)), S((36,)),
        ],
        compiler_params=pltpu.CompilerParams(
            collective_id=0, has_side_effects=True, vmem_limit_bytes=62 * 1024 * 1024
        ),
    )(
        query, keys, values, lengths, residual, out_proj, norm_gain.reshape(1, -1), expert_ids,
        gate_scores, w_gate[0], w_up[0], w_down[0],
    )


def solution(mesh):
    in_specs = (
        P(("expert", "tensor"), None),
        P(("expert", "tensor"), None, None, None),
        P(("expert", "tensor"), None, None, None),
        P(("expert", "tensor")),
        P("tensor", "expert"),
        P("expert", "tensor"),
        P("expert"),
        P(),
        P(),
        P("expert", "tensor", None),
        P("expert", "tensor", None),
        P("expert", "tensor", None),
    )
    out_specs = (P("tensor", "expert"), P("tensor", "expert"))
    fused = dict(mesh.shape) == {"expert": 16, "tensor": 2}
    return jax.shard_map(fused_body if fused else body, mesh=mesh, in_specs=in_specs, out_specs=out_specs, check_vma=False)
```

```python
import jax
import jax.numpy as jnp
from jax import lax
from jax.experimental import pallas as pl
from jax.experimental.pallas import tpu as pltpu
from jax.sharding import PartitionSpec as P

floor_value = -1e30
epsilon = 1e-06


def softmax_parts(queries, key_block, value_block, usable, score_scale):
    scores = (
        jnp.einsum("rkgd,rpkd->rkgp", queries, key_block, preferred_element_type=jnp.float32)
        * score_scale
    )
    usable_mask = usable[:, None, None, :]
    peak = jnp.max(jnp.where(usable_mask, scores, floor_value), axis=-1)
    raw_weights = jnp.where(usable_mask, jnp.exp(scores - peak[..., None]), 0.0)
    weight_sum = jnp.sum(raw_weights, axis=-1)
    weighted = jnp.einsum("rkgp,rpkd->rkgd", raw_weights, value_block.astype(jnp.float32))
    return (weight_sum, weighted)


def body(
    query,
    cache_keys,
    cache_values,
    lengths,
    residual,
    out_proj,
    norm_gain,
    expert_ids,
    gate_scores,
    w_gate,
    w_up,
    w_down,
):
    row_count, full_heads_width = query.shape
    cache_len = cache_keys.shape[1]
    kv_count = cache_keys.shape[2]
    head_size = cache_keys.shape[3]
    head_count = full_heads_width // head_size
    group_size = head_count // kv_count
    score_scale = head_size ** (-0.5)
    usable = jnp.arange(cache_len, dtype=jnp.int32)[None, :] < lengths[:, None]
    grouped = query.reshape(row_count, kv_count, group_size, head_size)
    weight_sum, weighted = softmax_parts(grouped, cache_keys, cache_values, usable, score_scale)
    context_rows_own = (
        (weighted / weight_sum[..., None]).astype(jnp.bfloat16).reshape(row_count, full_heads_width)
    )
    context = lax.all_to_all(context_rows_own, "tensor", split_axis=1, concat_axis=0, tiled=True)
    attn_part = jnp.dot(
        lax.all_gather(context, "expert", axis=0, tiled=True),
        out_proj.T,
        preferred_element_type=jnp.float32,
    )
    attn_share = lax.psum_scatter(attn_part, "tensor", scatter_dimension=0, tiled=True)
    hidden_state = residual.astype(jnp.float32) + attn_share
    squares = lax.psum(jnp.sum(hidden_state * hidden_state, axis=1), "expert")
    full_width = hidden_state.shape[1] * lax.axis_size("expert")
    scaled_share = (hidden_state * norm_gain.astype(jnp.float32)[None, :]).astype(jnp.bfloat16)
    scaled = lax.all_gather(
        lax.all_gather(scaled_share, "tensor", axis=0, tiled=True), "expert", axis=1, tiled=True
    )
    mean_all = lax.all_gather(squares / full_width, "tensor", axis=0, tiled=True)
    row_scale = lax.rsqrt(mean_all + epsilon)[:, None]
    experts_local = w_gate.shape[0]
    gate_weight = gate_scores.astype(jnp.float32)
    gate_weight = gate_weight / jnp.sum(gate_weight, axis=1, keepdims=True)
    mixed = None
    for local in range(experts_local):
        expert = lax.axis_index("expert") * experts_local + local
        weight = jnp.sum(jnp.where(expert_ids == expert, gate_weight, 0.0), axis=1, keepdims=True)
        gate_proj = row_scale * lax.dot_general(
            scaled, w_gate[local], (((1,), (1,)), ((), ())), preferred_element_type=jnp.float32
        )
        up_proj = row_scale * lax.dot_general(
            scaled, w_up[local], (((1,), (1,)), ((), ())), preferred_element_type=jnp.float32
        )
        activation = (jax.nn.silu(gate_proj) * up_proj).astype(jnp.bfloat16)
        part = weight * jnp.dot(activation, w_down[local], preferred_element_type=jnp.float32)
        mixed = part if mixed is None else mixed + part
    mixed = lax.psum_scatter(
        mixed.astype(jnp.bfloat16), "tensor", scatter_dimension=0, tiled=True
    )
    mixed_share = lax.psum_scatter(mixed, "expert", scatter_dimension=1, tiled=True)
    return (hidden_state.astype(jnp.bfloat16), mixed_share)


MESH = pl.DeviceIdType.MESH
NZ = 4
UP, DOWN, ACROSS, CORE = 0, 3, 6, 10


def remote(src, dst, send, recv, device):
    return pltpu.make_async_remote_copy(
        src_ref=src, dst_ref=dst, send_sem=send, recv_sem=recv, device_id=device, device_id_type=MESH
    )


class Gather:
    def __init__(self, bufs, sends, recvs, e, y):
        self.bufs, self.sends, self.recvs = bufs, sends, recvs
        self.e, self.y = e, y
        self.z, self.x, self.c = e // 4, (e // 2) % 2, e % 2
        self.ex = e + 2 * (1 - 2 * self.x)
        self.ec = e + 1 - 2 * self.c

    def copies(self, slot, sem, target):
        return [
            remote(
                b.at[slot], b.at[slot], self.sends.at[i, sem], self.recvs.at[i, sem], (target, self.y)
            )
            for i, b in enumerate(self.bufs)
        ]

    def start(self, slot, sem, target):
        for d in self.copies(slot, sem, target):
            d.start()

    def landed(self, slot, sem):
        for d in self.copies(slot, sem, self.ec):
            d.wait_recv()

    def sent(self, slot, sem):
        for d in self.copies(slot, sem, self.ec):
            d.wait_send()

    def slot(self, zz, xx, cc):
        return zz * 4 + xx * 2 + cc

    def forward(self, slot, zz):
        self.start(slot, ACROSS + zz, self.ex)
        self.start(slot, CORE + self.x * NZ + zz, self.ec)

    def run(self):
        z, x, c, e = self.z, self.x, self.c, self.e

        @pl.when(z < NZ - 1)
        def _():
            self.start(e, UP, e + 4)

        @pl.when(z > 0)
        def _():
            self.start(e, DOWN, e - 4)

        self.forward(e, z)
        for k in range(1, NZ):

            @pl.when(z - k >= 0)
            def _(k=k):
                slot = e - 4 * k
                self.landed(slot, UP + k - 1)
                if k < NZ - 1:

                    @pl.when(z < NZ - 1)
                    def _():
                        self.start(slot, UP + k, e + 4)

                self.forward(slot, z - k)

            @pl.when(z + k <= NZ - 1)
            def _(k=k):
                slot = e + 4 * k
                self.landed(slot, DOWN + k - 1)
                if k < NZ - 1:

                    @pl.when(z > 0)
                    def _():
                        self.start(slot, DOWN + k, e - 4)

                self.forward(slot, z + k)

        step = 1 - 2 * (z // 2)
        for j in range(NZ):
            zz = (z + step * j + NZ) % NZ
            slot = self.slot(zz, 1 - x, c)
            self.landed(slot, ACROSS + zz)
            self.start(slot, CORE + (1 - x) * NZ + zz, self.ec)

    def wait_core(self):
        for xx in range(2):
            for zz in range(NZ):
                self.landed(self.slot(zz, xx, 1 - self.c), CORE + xx * NZ + zz)

    def wait_sends(self):
        z, e = self.z, self.e
        for k in range(1, NZ):

            @pl.when((z < NZ - 1) & (z - (k - 1) >= 0))
            def _(k=k):
                self.sent(e - 4 * (k - 1), UP + k - 1)

            @pl.when((z > 0) & (z + k - 1 <= NZ - 1))
            def _(k=k):
                self.sent(e + 4 * (k - 1), DOWN + k - 1)

        for zz in range(NZ):
            self.sent(self.slot(zz, self.x, self.c), ACROSS + zz)
            for xx in range(2):
                self.sent(self.slot(zz, xx, self.c), CORE + xx * NZ + zz)


def nt_dot(a, b):
    return lax.dot_general(a, b, (((1,), (1,)), ((), ())), preferred_element_type=jnp.float32)


def layer_kernel(
    q_ref, k_hbm, v_hbm, len_ref, res_ref, wo_hbm, gain_ref, ids_ref, gates_ref,
    wg_hbm, wu_hbm, wd_hbm,
    out_ref,
    k_v, v_v, wo_v, wg_v, wu_v, wd_v, local_sems,
    lay, qlay, sblk, ctx, part, part_in, hid_all, sq_all,
    gate_acc, up_acc, act, own, fin, tmp, core_in, y0_out, y0_in, x1_out, x1_in, x0_out, x0_in,
    y1_out, y1_in, zout, up_in, down_in,
    c_send, c_recv, h_send, h_recv, p_send, p_recv, r_send, r_recv,
):
    f32, bf16 = jnp.float32, jnp.bfloat16
    e = lax.axis_index("expert")
    y = lax.axis_index("tensor")
    z, x, c = e // 4, (e // 2) % 2, e % 2
    ex, ec = e + 2 * (1 - 2 * x), e + 1 - 2 * c
    barrier = pltpu.get_barrier_semaphore()
    pairs = [(k_hbm, k_v), (v_hbm, v_v), (wo_hbm, wo_v), (wg_hbm, wg_v), (wu_hbm, wu_v), (wd_hbm, wd_v)]
    loads = [pltpu.make_async_copy(s, d, local_sems.at[i]) for i, (s, d) in enumerate(pairs)]
    loads[0].start()
    loads[1].start()
    for dev in ((ec, y), (ex, y), (e, 1 - y)):
        pl.semaphore_signal(barrier, inc=1, device_id=dev, device_id_type=MESH)

    @pl.when(z > 0)
    def _():
        pl.semaphore_signal(barrier, inc=1, device_id=(e - 4, y), device_id_type=MESH)

    @pl.when(z < NZ - 1)
    def _():
        pl.semaphore_signal(barrier, inc=1, device_id=(e + 4, y), device_id_type=MESH)

    rows = q_ref.shape[0]
    for h in range(64):
        qlay[h * 8 : h * 8 + rows, :] = q_ref[:, h * 128 : (h + 1) * 128].astype(f32)
    loads[0].wait()
    loads[1].wait()
    for d in loads[2:]:
        d.start()
    col = lax.broadcasted_iota(jnp.int32, (64, 512), 1)
    head = lax.broadcasted_iota(jnp.int32, (64, 512), 0)
    same = (col % 4) == (head // 16)
    for r in range(rows):
        q = qlay[pl.ds(r, 64, stride=8), :].astype(bf16)
        s = nt_dot(q, k_v[r]) * (128 ** -0.5)
        ok = same & ((col // 4) < len_ref[r])
        peak = jnp.max(jnp.where(ok, s, -1e30), axis=1, keepdims=True)
        w = jnp.where(ok, jnp.exp(s - peak), 0.0)
        total = jnp.sum(w, axis=1, keepdims=True)
        o = jnp.dot(w.astype(bf16), v_v[r], preferred_element_type=f32) / total
        for half in range(2):
            for j in range(4):
                h0 = half * 32 + j * 8
                lay[pl.ds(half * 128 + 4 * j + r, 8, stride=16), :] = o[h0 : h0 + 8]
    for half in range(2):
        for hh in range(8):
            t = (half * 8 + hh) * 16
            sblk[half, :, hh * 128 : (hh + 1) * 128] = lay[t : t + 16, :].astype(bf16)
    ctx[e, y] = sblk[y]
    pl.semaphore_wait(barrier, 4 + z * (NZ - 1 - z) // 2)

    swap = remote(sblk.at[1 - y], ctx.at[e, y], p_send.at[0], p_recv.at[0], (e, 1 - y))
    swap.start()
    swap.wait_recv()
    g1 = Gather([ctx], c_send, c_recv, e, y)
    g1.run()
    g1.wait_core()

    loads[2].wait()
    lhs = ctx.reshape(512, 1024)
    quarter = (lax.broadcasted_iota(jnp.int32, (512, 256), 0) % 16) // 4
    acc = jnp.zeros((512, 256), f32)
    for j in range(4):
        pj = nt_dot(lhs[...], wo_v[:, j * 1024 : (j + 1) * 1024])
        acc = jnp.where(quarter == j, pj, acc)
    folded = acc.reshape(32, 2, 8, 256)
    folded = (folded[:, 0] + folded[:, 1]).reshape(256, 256)
    low = (lax.broadcasted_iota(jnp.int32, (256, 256), 0) % 8) < 4
    folded = folded + jnp.where(low, pltpu.roll(folded, 252, 0), pltpu.roll(folded, 4, 0))
    folded = folded.reshape(16, 2, 8, 256)
    low3 = lax.broadcasted_iota(jnp.int32, (16, 8, 256), 1) < 4
    part[...] = jnp.where(low3, folded[:, 0], folded[:, 1]).reshape(2, 64, 256)
    psend = remote(part.at[1 - y], part_in, p_send.at[1], p_recv.at[1], (e, 1 - y))
    psend.start()
    psend.wait_recv()
    hidden = res_ref[...].astype(f32) + (part[y] + part_in[...])
    out_ref[0] = hidden
    hid_all[e, y] = (hidden * gain_ref[...].astype(f32).reshape(1, 256)).astype(bf16)
    ss = jnp.sum(hidden * hidden, axis=1, keepdims=True)
    place = lax.broadcasted_iota(jnp.int32, (64, 128), 0) + 64 * y
    lane = lax.broadcasted_iota(jnp.int32, (64, 128), 1)
    sq = jnp.sum(jnp.where(place == lane, ss, 0.0), axis=0, keepdims=True)
    sq_all[e, y] = jnp.broadcast_to(sq, (8, 128))
    hs = remote(hid_all.at[e, y], hid_all.at[e, y], p_send.at[2], p_recv.at[2], (e, 1 - y))
    qs = remote(sq_all.at[e, y], sq_all.at[e, y], p_send.at[3], p_recv.at[3], (e, 1 - y))
    hs.start()
    qs.start()
    hs.wait_recv()
    qs.wait_recv()
    g2 = Gather([hid_all, sq_all], h_send, h_recv, e, y)
    g2.run()
    loads[3].wait()
    loads[4].wait()

    def products(core, first):
        def step(n, _):
            rows_n = pl.ds(pl.multiple_of(n * 256, 256), 256)
            for wref, aref in ((wg_v, gate_acc), (wu_v, up_acc)):
                a = jnp.zeros((128, 256), f32) if first else aref[n]
                for j in range(8):
                    src = 2 * j + core
                    cols = pl.ds(pl.multiple_of(src * 256, 256), 256)
                    a = a + nt_dot(hid_all[src].reshape(128, 256), wref[rows_n, cols])
                aref[n] = a
            return 0

        lax.fori_loop(0, 3, step, 0)

    products(c, True)
    g2.wait_core()
    products(1 - c, False)
    total = jnp.sum(sq_all[...].reshape(32, 8, 128), axis=0)
    scale_row = lax.rsqrt(total[0:1] / 4096.0 + epsilon)
    eye = lax.broadcasted_iota(jnp.int32, (128, 128), 0) == lax.broadcasted_iota(jnp.int32, (128, 128), 1)
    scale = jnp.sum(jnp.where(eye, scale_row, 0.0), axis=1, keepdims=True)
    gw = gates_ref[...].astype(f32)
    gw = gw / jnp.sum(gw, axis=0, keepdims=True)
    weight_row = jnp.sum(jnp.where(ids_ref[...] == e, gw, 0.0), axis=0, keepdims=True)
    weight = jnp.sum(jnp.where(eye, weight_row, 0.0), axis=1, keepdims=True)
    for n in range(3):
        g = gate_acc[n] * scale
        u = up_acc[n] * scale
        act[:, n * 256 : (n + 1) * 256] = (g / (1.0 + jnp.exp(-g)) * u).astype(bf16)
    loads[5].wait()

    def block(zz, xx, cc):
        cols = pl.ds(pl.multiple_of((zz * 4 + xx * 2 + cc) * 256, 256), 256)
        p = jnp.dot(act[...], wd_v[:, cols], preferred_element_type=f32) * weight
        return p.reshape(2, 2, 32, 256)

    mirror = z // 2
    near_z = z + mirror * (3 - 2 * z)

    def far_first(i):
        o = (3, 2, 1 - near_z, near_z)[i]
        return o + mirror * (3 - 2 * o)

    def core_copy(b):
        return remote(tmp.at[b], core_in.at[b], r_send.at[b], r_recv.at[b], (ec, y))

    def y0_copy(b):
        return remote(y0_out.at[b], y0_in.at[b], r_send.at[8 + b], r_recv.at[8 + b], (e, 1 - y))

    def x1_copy(zz):
        return remote(x1_out.at[zz], x1_in.at[zz], r_send.at[16 + zz], r_recv.at[16 + zz], (ex, y))

    def x0_copy(zz):
        return remote(x0_out.at[zz], x0_in.at[zz], r_send.at[20 + zz], r_recv.at[20 + zz], (ex, y))

    def y1_copy(zz):
        return remote(y1_out.at[zz], y1_in.at[zz], r_send.at[24 + zz], r_recv.at[24 + zz], (e, 1 - y))

    def up_copy(zz):
        return remote(zout.at[zz], up_in.at[zz], r_send.at[28 + zz], r_recv.at[28 + zz], (e + 4, y))

    def down_copy(zz):
        return remote(zout.at[zz], down_in.at[zz], r_send.at[28 + zz], r_recv.at[32 + zz], (e - 4, y))

    for i in range(NZ):
        zz = far_first(i)
        for xx in (1 - x, x):
            b = xx * 4 + zz
            tmp[b] = block(zz, xx, 1 - c).astype(bf16)
            core_copy(b).start()

    for i in range(NZ):
        zz = far_first(i)
        for n, xx in enumerate((1 - x, x)):
            b = xx * 4 + zz
            own[b] = block(zz, xx, c)
            core_copy(b).wait_recv()
            own[b] = own[b] + core_in[b].astype(f32)
            y0_out[b] = own[b, 1 - y, 0].astype(bf16)
            y0_copy(b).start()
            if n == 0:
                x1_out[zz] = own[b, :, 1].astype(bf16)
                x1_copy(zz).start()

    for i in range(NZ):
        zz = far_first(i)
        far, near = (1 - x) * 4 + zz, x * 4 + zz
        x1_copy(zz).wait_recv()
        y1_out[zz] = (own[near, 1 - y, 1] + x1_in[zz, 1 - y].astype(f32)).astype(bf16)
        y1_copy(zz).start()
        y0_copy(far).wait_recv()
        x0_out[zz] = (own[far, y, 0] + y0_in[far].astype(f32)).astype(bf16)
        x0_copy(zz).start()

    for i in range(NZ):
        zz = far_first(i)
        near = x * 4 + zz
        y0_copy(near).wait_recv()
        x0_copy(zz).wait_recv()
        y1_copy(zz).wait_recv()
        fin[zz, 0] = own[near, y, 0] + y0_in[near].astype(f32) + x0_in[zz].astype(f32)
        fin[zz, 1] = own[near, y, 1] + x1_in[zz, y].astype(f32) + y1_in[zz].astype(f32)

        if i < NZ - 1:

            @pl.when(zz > z)
            def _():
                @pl.when(z > 0)
                def _():
                    up_copy(zz).wait_recv()
                    fin[zz] = fin[zz] + up_in[zz].astype(f32)

                zout[zz] = fin[zz].astype(bf16)
                up_copy(zz).start()

            @pl.when(zz < z)
            def _():
                @pl.when(z < NZ - 1)
                def _():
                    down_copy(zz).wait_recv()
                    fin[zz] = fin[zz] + down_in[zz].astype(f32)

                zout[zz] = fin[zz].astype(bf16)
                down_copy(zz).start()

    @pl.when(z > 0)
    def _():
        up_copy(z).wait_recv()
        fin[z] = fin[z] + up_in[z].astype(f32)

    @pl.when(z < NZ - 1)
    def _():
        down_copy(z).wait_recv()
        fin[z] = fin[z] + down_in[z].astype(f32)

    out_ref[1] = fin[z].reshape(64, 256)

    for d in (swap, psend, hs, qs):
        d.wait_send()
    g1.wait_sends()
    g2.wait_sends()
    for b in range(8):
        core_copy(b).wait_send()
        y0_copy(b).wait_send()
    for zz in range(NZ):
        x1_copy(zz).wait_send()
        x0_copy(zz).wait_send()
        y1_copy(zz).wait_send()
    for k in range(1, NZ):

        @pl.when(z + k <= NZ - 1)
        def _(k=k):
            up_copy(z + k).wait_send()

        @pl.when(z - k >= 0)
        def _(k=k):
            down_copy(z - k).wait_send()


def fused_body(
    query, cache_keys, cache_values, lengths, residual, out_proj, norm_gain, expert_ids, gate_scores,
    w_gate, w_up, w_down,
):
    f32, bf16 = jnp.float32, jnp.bfloat16
    rows = query.shape[0]
    keys = cache_keys.reshape(rows, 512, 128)
    values = cache_values.reshape(rows, 512, 128)
    vm = pl.BlockSpec(memory_space=pltpu.VMEM)
    hb = pl.BlockSpec(memory_space=pl.ANY)
    sm = pl.BlockSpec(memory_space=pltpu.SMEM)
    V, S = pltpu.VMEM, pltpu.SemaphoreType.DMA
    out = pl.pallas_call(
        layer_kernel,
        name="layer",
        out_shape=jax.ShapeDtypeStruct((2, 64, 256), f32),
        in_specs=[vm, hb, hb, sm, vm, hb, vm, vm, vm, hb, hb, hb],
        out_specs=vm,
        scratch_shapes=[
            V((rows, 512, 128), bf16), V((rows, 512, 128), bf16), V((256, 4096), bf16),
            V((768, 4096), bf16), V((768, 4096), bf16), V((768, 4096), bf16), S((6,)),
            V((256, 128), f32), V((512, 128), f32), V((2, 16, 1024), bf16), V((16, 2, 16, 1024), bf16),
            V((2, 64, 256), f32), V((64, 256), f32), V((16, 2, 64, 256), bf16), V((16, 2, 8, 128), f32),
            V((3, 128, 256), f32), V((3, 128, 256), f32), V((128, 768), bf16),
            V((8, 2, 2, 32, 256), f32), V((4, 2, 32, 256), f32),
            V((8, 2, 2, 32, 256), bf16), V((8, 2, 2, 32, 256), bf16),
            V((8, 32, 256), bf16), V((8, 32, 256), bf16),
            V((4, 2, 32, 256), bf16), V((4, 2, 32, 256), bf16),
            V((4, 32, 256), bf16), V((4, 32, 256), bf16),
            V((4, 32, 256), bf16), V((4, 32, 256), bf16),
            V((4, 2, 32, 256), bf16), V((4, 2, 32, 256), bf16), V((4, 2, 32, 256), bf16),
            S((1, 18)), S((1, 18)), S((2, 18)), S((2, 18)), S((4,)), S((4,)), S((36,)), S((36,)),
        ],
        compiler_params=pltpu.CompilerParams(
            collective_id=0, has_side_effects=True, vmem_limit_bytes=62 * 1024 * 1024
        ),
    )(
        query, keys, values, lengths, residual, out_proj, norm_gain, expert_ids.T,
        gate_scores.T, w_gate[0], w_up[0], w_down[0],
    )
    return (out[0].astype(bf16), out[1].astype(bf16))


def solution(mesh):
    in_specs = (
        P(("expert", "tensor"), None),
        P(("expert", "tensor"), None, None, None),
        P(("expert", "tensor"), None, None, None),
        P(("expert", "tensor")),
        P("tensor", "expert"),
        P("expert", "tensor"),
        P("expert"),
        P(),
        P(),
        P("expert", "tensor", None),
        P("expert", "tensor", None),
        P("expert", "tensor", None),
    )
    out_specs = (P("tensor", "expert"), P("tensor", "expert"))
    fused = dict(mesh.shape) == {"expert": 16, "tensor": 2}
    return jax.shard_map(fused_body if fused else body, mesh=mesh, in_specs=in_specs, out_specs=out_specs, check_vma=False)
```
